32 devices in a mesh: slab: 2 (over x), ang: 16 (over z, y, core).
Axes of the slice: x: 2, y: 2, z: 4, core: 2. Of those that a mesh axis runs over, the one named last changes fastest.
Arguments:
- raw_counts: float32 [4096, 8, 2048], P('ang', 'slab'), parts along dimension 1, may hold values from 500 to 8000
- dark_frames: float32 [4, 8, 2048], P(None, 'slab'), parts along dimension 1, may hold values from 100 to 400
- flat_frames: float32 [8, 8, 2048], P(None, 'slab'), parts along dimension 1, may hold values from 8000 to 12000
- dark_index: int32 [4096], P('ang'), may hold values from 0 to 3
- flat_index: int32 [4096], P('ang'), may hold values from 0 to 7
- center_offset: int32 [1], replicated, may hold values from 64 to 255
- blend_width: int32 [1], replicated, may hold values from 2 to 128
- stripe_gain: float32 [1025], replicated, may hold values from 0.25 to 1
- ramp_window: float32 [2049], replicated, may hold values from 0.5 to 2
Outputs:
- filtered: float32 [2048, 8, 4096], P('ang', 'slab'), parts along dimension 1
The draws below stay inside these ranges and needn't reach their ends.
There are 2 independent parts, one for each index of `slab`. The reference program is written for one: setup_inputs(seed, part) draws one part's arguments, and reference() takes and returns one part's arrays. A program takes and returns all parts, laid end to end along the dimension named above; an argument that names none is the same for every part. Nothing has to cross between parts.
Inputs may be any that keep to these rules, and one draw needn't show every extreme that they name: `blend_width`: the blend width never exceeds twice the center offset.
All inputs are finite; a program needn't handle non-finite values.
Results may differ from the reference program's by a relative error of at most 0.00075.
Values sent between devices are 32-bit elements; how exact they have to be, the bound alone decides.
No kernel may reach another device: no remote copies, remote signals or barrier semaphores. Data moves between devices by JAX's collectives and lax.ppermute only.
A program may use at most 256 MiB of HBM per device.

```python
import math
import jax
import jax.numpy as jnp
from jax import lax

PROJ = 4096
DET = 2048
ROWS = 4
NDARK = 4
NFLAT = 8
VIEWS = 2048


def touch_ends(drawn, own_key, smallest, top_value):
    longest = drawn.shape.index(max(drawn.shape))
    spots = []
    for shift in (0, 1):
        where = [jax.random.randint(jax.random.fold_in(own_key, axis), (), 0, length) for axis, length in enumerate(drawn.shape)]
        where[longest] = (where[longest] + shift) % drawn.shape[longest]
        spots.append(tuple(where))
    return drawn.at[spots[0]].set(smallest).at[spots[1]].set(top_value)


def level_of(rng, extent, shards, low, top_value):
    def one(position, blocks):
        heights = jax.random.uniform(jax.random.fold_in(jax.random.fold_in(rng, 6), position), (blocks,), jnp.float32, low / len(shards), top_value / len(shards))
        return jnp.repeat(jnp.exp(heights), extent[position] // blocks).reshape((-1,) + (1,) * (len(extent) - position - 1))

    factor_of = one(*shards[0])
    for cut in shards[1:]:
        factor_of = factor_of * one(*cut)
    return factor_of


def setup_inputs(seed: int = 0, part: int = 0) -> dict:
    key_list = jax.random.split(jax.random.key(seed), 10)
    part_keys = jax.random.split(jax.random.fold_in(key_list[9], part), 10)
    return {
        "raw_counts": jnp.clip(jnp.exp(math.log(8000.0) - 2.7725887 * jax.random.uniform(part_keys[0], (PROJ, ROWS, DET), jnp.float32) ** level_of(part_keys[0], (PROJ, ROWS, DET), ((0, 16),), -0.2, 0.2)), 500.0, 8000.0),
        "dark_frames": jnp.clip(jax.random.uniform(part_keys[1], (NDARK, ROWS, DET), jnp.float32, 100.0, 400.0), 100.0, 400.0),
        "flat_frames": jnp.clip(jax.random.uniform(part_keys[2], (NFLAT, ROWS, DET), jnp.float32, 8000.0, 12000.0), 8000.0, 12000.0),
        "dark_index": touch_ends(jax.random.randint(key_list[3], (PROJ,), 0, NDARK), jax.random.fold_in(key_list[3], 1), 0, NDARK - 1).astype(jnp.int32),
        "flat_index": touch_ends(jax.random.randint(key_list[4], (PROJ,), 0, NFLAT), jax.random.fold_in(key_list[4], 1), 0, NFLAT - 1).astype(jnp.int32),
        "center_offset": jax.random.randint(key_list[5], (1,), DET // 32, DET // 8).astype(jnp.int32),
        "blend_width": jax.random.randint(key_list[6], (1,), 2, DET // 16 + 1).astype(jnp.int32),
        "stripe_gain": jnp.clip(jnp.exp(jax.random.uniform(key_list[7], (VIEWS // 2 + 1,), jnp.float32, math.log(0.25), math.log(1.0))), 0.25, 1.0),
        "ramp_window": jnp.clip(jnp.exp(jax.random.uniform(key_list[8], (DET + 1,), jnp.float32, math.log(0.5), math.log(2.0))), 0.5, 2.0),
    }


def stitch(direct, partner, offset, blend):
    zeros = jnp.zeros_like(direct)
    padded_direct = jnp.concatenate([zeros, direct, zeros], axis=2)
    padded_partner = jnp.concatenate([zeros, partner[:, :, ::-1], zeros], axis=2)
    offset = offset.astype(jnp.int32)
    direct_part = lax.dynamic_slice_in_dim(padded_direct, offset, 2 * DET, 2)
    partner_part = lax.dynamic_slice_in_dim(padded_partner, DET - 1 - offset, 2 * DET, 2)
    positions = jnp.arange(2 * DET).astype(jnp.float32)
    spread = blend.astype(jnp.float32)
    weight = jnp.clip((positions - DET + 0.5 * spread) / spread, 0.0, 1.0)
    return (1.0 - weight) * partner_part + weight * direct_part


def reference(raw_counts, dark_frames, flat_frames, dark_index, flat_index, center_offset, blend_width, stripe_gain, ramp_window):
    dark_pick = dark_frames[dark_index]
    flat_pick = flat_frames[flat_index]
    sinogram = -jnp.log((raw_counts - dark_pick) / (flat_pick - dark_pick))
    stitched = stitch(sinogram[:VIEWS], sinogram[VIEWS:], center_offset[0], blend_width[0])
    spectrum = jnp.fft.rfft(stitched, axis=0)
    destriped = jnp.fft.irfft(spectrum * stripe_gain[:, None, None], n=VIEWS, axis=0)
    frequency = jnp.arange(DET + 1).astype(jnp.float32)
    response = 4.0 * frequency / (2 * DET) * ramp_window
    filtered = jnp.fft.irfft(jnp.fft.rfft(destriped, axis=2) * response, n=2 * DET, axis=2)
    return filtered.astype(jnp.float32)
```

```python
import functools

import jax
import jax.numpy as jnp
import numpy as np
from jax import lax
from jax.experimental import pallas as pl
from jax.experimental.pallas import tpu as pltpu
from jax.sharding import PartitionSpec as P

DET = 2048
VIEWS = 2048
STITCH = 2 * DET
EDGE = 64
TILE = 256
CHUNKS = 2
VMEM_BYTES = 56 * 1024 * 1024

precise = lax.Precision.HIGHEST


def select_frames(index, frames):
    choices_onehot = (
        index[:, None] == jnp.arange(frames.shape[0], dtype=jnp.int32)[None, :]
    ).astype(jnp.float32)
    picked = jnp.dot(choices_onehot, frames.reshape(frames.shape[0], -1), precision=precise)
    return picked.reshape((index.shape[0],) + frames.shape[1:])


def impulse(gains, length):
    inner = 64
    period = length // inner
    outer = period // 2
    phase = lambda rows, cols, whole: 2.0 * np.pi * (np.outer(rows, cols) % whole) / whole
    first = phase(np.arange(period), np.arange(outer), period)
    turn = phase(np.arange(period), np.arange(inner), length)
    last = phase(np.arange(inner), np.arange(inner), inner)
    table = lambda values: jnp.asarray(values.astype(np.float32))
    doubled = np.full((length // 2,), 2.0 / length, np.float32)
    doubled[0] = 1.0 / length
    coefs = (gains[:-1] * doubled).reshape(outer, inner)
    real = jnp.dot(table(np.cos(first)), coefs, precision=precise)
    imag = jnp.dot(table(np.sin(first)), coefs, precision=precise)
    cos_turn, sin_turn = table(np.cos(turn)), table(np.sin(turn))
    turned_real = real * cos_turn - imag * sin_turn
    turned_imag = real * sin_turn + imag * cos_turn
    contract = (((1,), (1,)), ((), ()))
    line = lax.dot_general(table(np.cos(last)), turned_real, contract, precision=precise)
    line = line - lax.dot_general(table(np.sin(last)), turned_imag, contract, precision=precise)
    signs = table(np.where(np.arange(period) % 2 == 0, 1.0, -1.0) / length)
    return (line + signs[None, :] * gains[-1]).reshape(length)


def ring_lines(line):
    quarter = line.shape[0] // 4
    q = line.reshape(4, quarter)
    even, odd = q[0] + q[2], q[1] + q[3]
    cyclic = 0.25 * (even + odd)
    negative = 0.25 * (even - odd)
    wide = 0.5 * jnp.concatenate([q[0] - q[2], q[1] - q[3]])
    return jnp.concatenate([cyclic, cyclic, negative, -negative, wide, -wide])[None, :]


def ring_spans(quarter):
    return ((0, quarter), (2 * quarter, quarter), (4 * quarter, 2 * quarter))


def band_kernel(line_ref, high_ref, low_ref):
    quarter = line_ref.shape[1] // 8
    step = 32
    for start, size in ring_spans(quarter):
        row = line_ref[:, start : start + 2 * size]
        wide = jnp.broadcast_to(row, (step, 2 * size))
        for top in range(0, TILE, step):
            shifted = pltpu.roll(wide, size - TILE + top, 1, stride=1, stride_axis=0)
            high = shifted.astype(jnp.bfloat16)
            low = (shifted - high.astype(jnp.float32)).astype(jnp.bfloat16)
            high_ref[top : top + step, start : start + 2 * size] = high
            low_ref[top : top + step, start : start + 2 * size] = low


def bands(line):
    shape = jax.ShapeDtypeStruct((TILE, line.shape[1]), jnp.bfloat16)
    return pl.pallas_call(
        band_kernel,
        out_shape=(shape, shape),
        compiler_params=pltpu.CompilerParams(vmem_limit_bytes=VMEM_BYTES),
        cost_estimate=pl.CostEstimate(
            flops=4 * TILE * line.shape[1],
            bytes_accessed=4 * TILE * line.shape[1],
            transcendentals=0,
        ),
        name="bands",
    )(line)


def split(values):
    high = values.astype(jnp.bfloat16)
    return high, (values - high.astype(jnp.float32)).astype(jnp.bfloat16)


def dot32(left, right, contract):
    return lax.dot_general(left, right, (contract, ((), ())), preferred_element_type=jnp.float32)


def prepare_kernel(scalars, sino_ref, weight_ref, out_ref):
    count = out_ref.shape[0]
    width = out_ref.shape[3]
    weight = weight_ref[...]
    values = sino_ref[0]
    shift = scalars[1]

    def emit(turned):
        rolled = pltpu.roll(turned, shift, 1) * weight
        for block in range(count):
            out_ref[block, 0] = rolled[:, block * width : (block + 1) * width]

    @pl.when(scalars[0] == 0)
    def _():
        emit(values)

    @pl.when(scalars[0] != 0)
    def _():
        rows = values.shape[0]
        lanes = 127 - lax.broadcasted_iota(jnp.int32, (rows, 128), 1)
        pieces = [
            jnp.take_along_axis(values[:, start : start + 128], lanes, axis=1)
            for start in range(DET - 128, -1, -128)
        ]
        emit(jnp.concatenate(pieces, axis=1))


def prepare(scalars, sino, weight, start, rows, count):
    share = sino.shape[1]
    width = DET // count
    return pl.pallas_call(
        prepare_kernel,
        out_shape=jax.ShapeDtypeStruct((count, rows, share, width), jnp.float32),
        grid_spec=pltpu.PrefetchScalarGridSpec(
            num_scalar_prefetch=1,
            grid=(rows,),
            in_specs=[
                pl.BlockSpec((1, share, DET), lambda r, s: (r + start, 0, 0)),
                pl.BlockSpec((1, DET), lambda r, s: (0, 0)),
            ],
            out_specs=pl.BlockSpec((count, 1, share, width), lambda r, s: (0, r, 0, 0)),
        ),
        compiler_params=pltpu.CompilerParams(vmem_limit_bytes=VMEM_BYTES),
        cost_estimate=pl.CostEstimate(
            flops=8 * rows * share * DET, bytes_accessed=8 * rows * share * DET, transcendentals=0
        ),
        name="prepare",
    )(scalars, sino, weight)


def destripe_kernel(x_ref, high_ref, low_ref, y_ref):
    width = x_ref.shape[3]
    quarter = VIEWS // 4
    x = x_ref[...].reshape(4, quarter, width)
    even, odd = x[0] + x[2], x[1] + x[3]
    wide = jnp.concatenate([x[0] - x[2], x[1] - x[3]], axis=0)
    results = []
    for (start, size), ring in zip(ring_spans(quarter), (even + odd, even - odd, wide)):
        ring_high, ring_low = split(ring)
        pieces = []
        for block in range(size // TILE):
            left = start + size - TILE - TILE * block
            band_high = high_ref[:, left : left + size]
            band_low = low_ref[:, left : left + size]
            piece = dot32(band_high, ring_high, ((1,), (0,)))
            piece += dot32(band_high, ring_low, ((1,), (0,)))
            piece += dot32(band_low, ring_high, ((1,), (0,)))
            pieces.append(piece)
        results.append(jnp.concatenate(pieces, axis=0))
    cyclic, negative, wide = results
    both = jnp.concatenate([cyclic + negative, cyclic - negative], axis=0)
    whole = jnp.concatenate([both + wide, both - wide], axis=0)
    y_ref[...] = whole.reshape(y_ref.shape)


def destripe(x, high, low, devices):
    count, rows, share, width = x.shape
    views = VIEWS // devices
    band = pl.BlockSpec(high.shape, lambda r: (0, 0), pipeline_mode=pl.Buffered(1))
    return pl.pallas_call(
        destripe_kernel,
        out_shape=jax.ShapeDtypeStruct((devices, rows, views, width), jnp.float32),
        grid=(rows,),
        in_specs=[pl.BlockSpec((count, 1, share, width), lambda r: (0, r, 0, 0)), band, band],
        out_specs=pl.BlockSpec((devices, 1, views, width), lambda r: (0, r, 0, 0)),
        compiler_params=pltpu.CompilerParams(vmem_limit_bytes=VMEM_BYTES),
        cost_estimate=pl.CostEstimate(
            flops=3 * 2 * rows * width * VIEWS * 768,
            bytes_accessed=8 * rows * VIEWS * width + 4 * high.size,
            transcendentals=0,
        ),
        name="destripe",
    )(x, high, low)


def ramp_kernel(x_ref, high_ref, low_ref, y_ref):
    blocks, rows, views, width = x_ref.shape
    half = blocks // 2
    depth = rows * views
    pieces = [x_ref[block].reshape(depth, width) for block in range(blocks)]
    direct = jnp.concatenate(pieces[:half], axis=1)
    partner = jnp.concatenate(pieces[half:], axis=1)
    place = lax.broadcasted_iota(jnp.int32, (1, DET), 1)
    direct_sign = jnp.where(place >= DET - EDGE, 1.0, -1.0)
    partner_sign = jnp.where(place < EDGE, -1.0, 1.0)
    total = direct + partner
    wide = direct * direct_sign + partner * partner_sign
    quarter = DET // 2
    left_half, right_half = total[:, :quarter], total[:, quarter:]
    results = []
    rings = (left_half + right_half, left_half - right_half, wide)
    for (start, size), ring in zip(ring_spans(quarter), rings):
        ring_high, ring_low = split(ring)
        pieces = []
        for block in range(size // TILE):
            left = start + size - TILE - TILE * block
            band_high = high_ref[:, left : left + size]
            band_low = low_ref[:, left : left + size]
            piece = dot32(ring_high, band_high, ((1,), (1,)))
            piece += dot32(ring_low, band_high, ((1,), (1,)))
            piece += dot32(ring_high, band_low, ((1,), (1,)))
            pieces.append(piece)
        results.append(jnp.concatenate(pieces, axis=1))
    cyclic, negative, wide = results
    both = jnp.concatenate([cyclic + negative, cyclic - negative], axis=1)
    y_ref[:, :, :DET] = (both + wide).reshape(rows, views, DET)
    y_ref[:, :, DET:] = (both - wide).reshape(rows, views, DET)


def ramp(x, high, low):
    blocks, rows, views, width = x.shape
    return pl.pallas_call(
        ramp_kernel,
        out_shape=jax.ShapeDtypeStruct((rows, views, STITCH), jnp.float32),
        compiler_params=pltpu.CompilerParams(vmem_limit_bytes=VMEM_BYTES),
        cost_estimate=pl.CostEstimate(
            flops=3 * 2 * rows * views * STITCH * 1536,
            bytes_accessed=8 * rows * views * STITCH + 4 * high.size,
            transcendentals=0,
        ),
        name="ramp",
    )(x, high, low)


def shards(
    raw_counts,
    dark_frames,
    flat_frames,
    dark_index,
    flat_index,
    center_offset,
    blend_width,
    stripe_gain,
    ramp_window,
):
    devices = lax.axis_size("ang")
    half = devices // 2
    rows = raw_counts.shape[1]
    upper = lax.axis_index("ang") >= half
    offset = center_offset[0]
    spread = blend_width[0].astype(jnp.float32)

    dark_pick = select_frames(dark_index, dark_frames)
    flat_pick = select_frames(flat_index, flat_frames)
    sino = -jnp.log((raw_counts - dark_pick) / (flat_pick - dark_pick))
    sino = sino.transpose(1, 0, 2)

    place = jnp.arange(DET, dtype=jnp.int32)
    first_low = jnp.where(upper, offset + 1, DET - offset)
    position = jnp.where(place >= first_low, place, place + DET).astype(jnp.float32)
    weight = jnp.clip((position - DET + 0.5 * spread) / spread, 0.0, 1.0)
    weight = jnp.where(upper, 1.0 - weight, weight)[None, :]
    scalars = jnp.stack([upper.astype(jnp.int32), first_low.astype(jnp.int32)])

    frequency = jnp.arange(DET + 1).astype(jnp.float32)
    stripe_line = ring_lines(impulse(stripe_gain, VIEWS))
    ramp_line = ring_lines(impulse(4.0 * frequency / STITCH * ramp_window, STITCH))
    stripe_high, stripe_low = bands(stripe_line)
    ramp_high, ramp_low = bands(ramp_line)

    groups = [list(range(half)), list(range(half, devices))]
    chunk = rows // CHUNKS
    outputs = []
    for start in range(0, rows, chunk):
        sent = prepare(scalars, sino, weight, start, chunk, half)
        columns = lax.all_to_all(sent, "ang", 0, 0, axis_index_groups=groups, tiled=True)
        destriped = destripe(columns, stripe_high, stripe_low, devices)
        view_rows = lax.all_to_all(destriped, "ang", 0, 0, tiled=True)
        outputs.append(ramp(view_rows, ramp_high, ramp_low))
    filtered = jnp.concatenate(outputs, axis=0)
    return filtered.transpose(1, 0, 2)


def solution(mesh):
    in_specs = (
        P("ang", "slab", None),
        P(None, "slab", None),
        P(None, "slab", None),
        P("ang"),
        P("ang"),
        P(),
        P(),
        P(),
        P(),
    )
    out_specs = P("ang", "slab", None)
    return jax.shard_map(shards, mesh=mesh, in_specs=in_specs, out_specs=out_specs, check_vma=False)
```

```python
import functools

import jax
import jax.numpy as jnp
import numpy as np
from jax import lax
from jax.experimental import pallas as pl
from jax.experimental.pallas import tpu as pltpu
from jax.sharding import PartitionSpec as P

DET = 2048
VIEWS = 2048
STITCH = 2 * DET
EDGE = 64
TILE = 256
CHUNKS = 2
STEP = 128
UNROLL = 4
STRIPE_UNROLL = 2
RAMP_UNROLL = 4
MIB = 1024 * 1024
RAMP_VMEM = 48 * MIB
STRIPE_VMEM = 48 * MIB
PREPARE_VMEM = 56 * MIB

precise = lax.Precision.HIGHEST


def impulse(gains, length):
    inner = 64
    period = length // inner
    outer = period // 2
    phase = lambda rows, cols, whole: 2.0 * np.pi * (np.outer(rows, cols) % whole) / whole
    first = phase(np.arange(period), np.arange(outer), period)
    turn = phase(np.arange(period), np.arange(inner), length)
    last = phase(np.arange(inner), np.arange(inner), inner)
    table = lambda values: jnp.asarray(values.astype(np.float32))
    doubled = np.full((length // 2,), 2.0 / length, np.float32)
    doubled[0] = 1.0 / length
    coefs = (gains[:-1] * doubled).reshape(outer, inner)
    real = jnp.dot(table(np.cos(first)), coefs, precision=precise)
    imag = jnp.dot(table(np.sin(first)), coefs, precision=precise)
    cos_turn, sin_turn = table(np.cos(turn)), table(np.sin(turn))
    turned_real = real * cos_turn - imag * sin_turn
    turned_imag = real * sin_turn + imag * cos_turn
    contract = (((1,), (1,)), ((), ()))
    line = lax.dot_general(table(np.cos(last)), turned_real, contract, precision=precise)
    line = line - lax.dot_general(table(np.sin(last)), turned_imag, contract, precision=precise)
    signs = table(np.where(np.arange(period) % 2 == 0, 1.0, -1.0) / length)
    return (line + signs[None, :] * gains[-1]).reshape(length)


def ring_lines(line):
    quarter = line.shape[0] // 4
    q = line.reshape(4, quarter)
    even, odd = q[0] + q[2], q[1] + q[3]
    cyclic = 0.25 * (even + odd)
    negative = 0.25 * (even - odd)
    wide = 0.5 * jnp.concatenate([q[0] - q[2], q[1] - q[3]])
    return jnp.concatenate([cyclic, cyclic, negative, -negative, wide, -wide])[None, :]


def ring_spans(quarter):
    return ((0, quarter), (2 * quarter, quarter), (4 * quarter, 2 * quarter))


def band_kernel(line_ref, high_ref, low_ref, *, flip):
    quarter = line_ref.shape[1] // 8
    step = TILE if flip else 32
    for start, size in ring_spans(quarter):
        row = line_ref[:, start : start + 2 * size]
        wide = jnp.broadcast_to(row, (step, 2 * size))
        for top in range(0, TILE, step):
            shifted = pltpu.roll(wide, size - TILE + top, 1, stride=1, stride_axis=0)
            if flip:
                shifted = shifted.T
            high = shifted.astype(jnp.bfloat16)
            low = (shifted - high.astype(jnp.float32)).astype(jnp.bfloat16)
            if flip:
                place = (slice(start, start + 2 * size), slice(None))
            else:
                place = (slice(top, top + step), slice(start, start + 2 * size))
            high_ref[place] = high
            low_ref[place] = low


def bands(line, flip):
    size = line.shape[1]
    shape = jax.ShapeDtypeStruct((size, TILE) if flip else (TILE, size), jnp.bfloat16)
    return pl.pallas_call(
        functools.partial(band_kernel, flip=flip),
        out_shape=(shape, shape),
        compiler_params=pltpu.CompilerParams(vmem_limit_bytes=40 * MIB),
        cost_estimate=pl.CostEstimate(
            flops=4 * TILE * size, bytes_accessed=4 * TILE * size, transcendentals=0
        ),
        name="bands",
    )(line)


def split(values):
    high = values.astype(jnp.bfloat16)
    return high, (values - high.astype(jnp.float32)).astype(jnp.bfloat16)


def dot32(left, right, contract):
    return lax.dot_general(left, right, (contract, ((), ())), preferred_element_type=jnp.float32)


def prepare_kernel(
    scalars, dark_index, flat_index, raw_ref, dark_ref, flat_ref, weight_ref, out_ref, turned_ref, *, start
):
    count, rows, share, width = out_ref.shape
    blocks = DET // 128
    lines = dark_ref.shape[1]
    total = lines // blocks
    group = 8 // total if total < 8 else 1
    upper, shift = scalars[0], scalars[1]
    turn, jump = shift % 128, shift // 128
    lane = lax.broadcasted_iota(jnp.int32, (share, 128), 1)
    back = (lane + (128 - turn)) & 127
    pick = jnp.where(upper != 0, 127 - back, back)
    first = pl.program_id(0) * share

    def logs(eight, carry):
        pieces = []
        for one in range(8):
            view = eight * 8 + one
            dark = dark_ref[dark_index[first + view]]
            flat = flat_ref[flat_index[first + view]]
            raw = raw_ref[pl.ds(pl.multiple_of(view * lines, 8), lines), :]
            pieces.append(jnp.log(flat - dark) - jnp.log(raw - dark))
        top = pl.ds(pl.multiple_of(eight * 8, 8), 8)
        stacked = jnp.stack(pieces)
        for part in range(blocks // group):
            square = stacked[:, part * group * total : (part + 1) * group * total]
            square = pltpu.einshape("abc->bac", square)
            for inner in range(group):
                for row in range(rows):
                    turned_ref[row, part * group + inner, top, :] = square[inner * total + start + row]
        return carry

    lax.fori_loop(0, share // 8, logs, 0)

    def turned(block):
        source = jnp.where(upper != 0, blocks - 1 - block, block)
        return [jnp.take_along_axis(turned_ref[row, source], pick, axis=1) for row in range(rows)]

    def body(block, before):
        now = turned(block)
        target = (block + jump) % blocks
        place = pl.ds(pl.multiple_of(target * 128, 128), 128)
        weight = weight_ref[:, place]
        for row in range(rows):
            mixed = jnp.where(lane >= turn, now[row], before[row]) * weight
            if width >= 128:
                per = width // 128
                inside = pl.ds(pl.multiple_of((target % per) * 128, 128), 128)
                out_ref[target // per, row, :, inside] = mixed
            else:
                per = 128 // width
                for part in range(per):
                    out_ref[target * per + part, row] = mixed[:, part * width : (part + 1) * width]
        return now

    lax.fori_loop(0, blocks, body, turned(blocks - 1), unroll=UNROLL)


def prepare(scalars, indices, raw, dark, flat, weight, start, rows, count):
    share = indices[0].shape[0]
    width = DET // count
    step = min(share, STEP)
    lines = raw.shape[0] // share
    return pl.pallas_call(
        functools.partial(prepare_kernel, start=start),
        out_shape=jax.ShapeDtypeStruct((count, rows, share, width), jnp.float32),
        grid_spec=pltpu.PrefetchScalarGridSpec(
            num_scalar_prefetch=3,
            grid=(share // step,),
            in_specs=[
                pl.BlockSpec((lines * step, 128), lambda p, *s: (p, 0)),
                pl.BlockSpec(dark.shape, lambda p, *s: (0, 0, 0)),
                pl.BlockSpec(flat.shape, lambda p, *s: (0, 0, 0)),
                pl.BlockSpec((1, DET), lambda p, *s: (0, 0)),
            ],
            out_specs=pl.BlockSpec((count, rows, step, width), lambda p, *s: (0, 0, p, 0)),
            scratch_shapes=[pltpu.VMEM((rows, DET // 128, step, 128), jnp.float32)],
        ),
        compiler_params=pltpu.CompilerParams(vmem_limit_bytes=PREPARE_VMEM),
        cost_estimate=pl.CostEstimate(
            flops=20 * rows * share * DET,
            bytes_accessed=4 * rows * share * DET + 4 * raw.size,
            transcendentals=2 * raw.size,
        ),
        name="prepare",
    )(scalars, *indices, raw, dark, flat, weight)


def band_place(start, size, block):
    return pl.ds(pl.multiple_of(start + size - TILE - TILE * block, TILE), size)


def destripe_kernel(x_ref, high_ref, low_ref, y_ref, full_ref):
    width = x_ref.shape[3]
    quarter = VIEWS // 4
    x = x_ref[...].reshape(4, quarter, width)
    even, odd = x[0] + x[2], x[1] + x[3]
    wide = jnp.concatenate([x[0] - x[2], x[1] - x[3]], axis=0)
    rings = [split(ring) for ring in (even + odd, even - odd, wide)]
    spans = ring_spans(quarter)

    def product(ring, block):
        place = band_place(*spans[ring], block)
        high, low = high_ref[:, place], low_ref[:, place]
        ring_high, ring_low = rings[ring]
        piece = dot32(high, ring_high, ((1,), (0,)))
        piece += dot32(high, ring_low, ((1,), (0,)))
        return piece + dot32(low, ring_high, ((1,), (0,)))

    count = quarter // TILE

    def body(block, carry):
        cyclic, negative = product(0, block), product(1, block)
        for part, both in enumerate((cyclic + negative, cyclic - negative)):
            wide = product(2, block + part * count)
            top = pl.multiple_of(part * quarter + block * TILE, TILE)
            full_ref[pl.ds(top, TILE), :] = both + wide
            full_ref[pl.ds(top + 2 * quarter, TILE), :] = both - wide
        return carry

    lax.fori_loop(0, count, body, 0, unroll=STRIPE_UNROLL)
    y_ref[...] = full_ref[...].reshape(y_ref.shape)


def destripe(x, high, low, devices):
    count, rows, share, width = x.shape
    views = VIEWS // devices
    band = pl.BlockSpec(high.shape, lambda r: (0, 0), pipeline_mode=pl.Buffered(1))
    return pl.pallas_call(
        destripe_kernel,
        out_shape=jax.ShapeDtypeStruct((devices, rows, views, width), jnp.float32),
        grid=(rows,),
        in_specs=[pl.BlockSpec((count, 1, share, width), lambda r: (0, r, 0, 0)), band, band],
        out_specs=pl.BlockSpec((devices, 1, views, width), lambda r: (0, r, 0, 0)),
        scratch_shapes=[pltpu.VMEM((VIEWS, width), jnp.float32)],
        compiler_params=pltpu.CompilerParams(vmem_limit_bytes=STRIPE_VMEM),
        cost_estimate=pl.CostEstimate(
            flops=3 * 2 * rows * width * VIEWS * 768,
            bytes_accessed=8 * rows * VIEWS * width + 4 * high.size,
            transcendentals=0,
        ),
        name="destripe",
    )(x, high, low)


def ramp_kernel(x_ref, high_ref, low_ref, *refs, total):
    *done_refs, y_ref = refs
    blocks, rows, views, width = x_ref.shape
    half = blocks // 2
    depth = rows * views
    pieces = [x_ref[block].reshape(depth, width) for block in range(blocks)]
    direct = jnp.concatenate(pieces[:half], axis=1)
    partner = jnp.concatenate(pieces[half:], axis=1)
    place = lax.broadcasted_iota(jnp.int32, (1, DET), 1)
    direct_sign = jnp.where(place >= DET - EDGE, 1.0, -1.0)
    partner_sign = jnp.where(place < EDGE, -1.0, 1.0)
    added = direct + partner
    wide = direct * direct_sign + partner * partner_sign
    quarter = DET // 2
    left_half, right_half = added[:, :quarter], added[:, quarter:]
    rings = [split(ring) for ring in (left_half + right_half, left_half - right_half, wide)]
    spans = ring_spans(quarter)

    def product(ring, block):
        place = band_place(*spans[ring], block)
        high, low = high_ref[place, :], low_ref[place, :]
        ring_high, ring_low = rings[ring]
        piece = dot32(ring_high, high, ((1,), (0,)))
        piece += dot32(ring_low, high, ((1,), (0,)))
        return piece + dot32(ring_high, low, ((1,), (0,)))

    def emit(left, values):
        place = pl.ds(pl.multiple_of(left, TILE), TILE)
        values = values.reshape(rows, views, TILE)
        if not total:
            y_ref[:, :, place] = values
            return
        lines = [ref[row, :, place] for ref in done_refs for row in range(ref.shape[0])]
        lines += [values[row] for row in range(rows)]
        parts = TILE // 128
        square = jnp.stack([line[:, part * 128 : (part + 1) * 128] for part in range(parts) for line in lines])
        place = pl.ds(pl.multiple_of(left // 128 * total, parts * total), parts * total)
        y_ref[:, place, :] = pltpu.einshape("abc->bac", square)

    count = quarter // TILE

    def body(block, carry):
        cyclic, negative = product(0, block), product(1, block)
        for part, both in enumerate((cyclic + negative, cyclic - negative)):
            wide = product(2, block + part * count)
            left = part * quarter + block * TILE
            emit(left, both + wide)
            emit(left + DET, both - wide)
        return carry

    lax.fori_loop(0, count, body, 0, unroll=RAMP_UNROLL)


def ramp(x, high, low, done=(), total=0):
    blocks, rows, views, width = x.shape
    step = min(views, max(128 // rows, 8))
    if total:
        shape = (views, STITCH // 128 * total, 128)
        out_spec = pl.BlockSpec((step,) + shape[1:], lambda p: (p, 0, 0))
    else:
        shape = (rows, views, STITCH)
        out_spec = pl.BlockSpec((rows, step, STITCH), lambda p: (0, p, 0))
    band = pl.BlockSpec(high.shape, lambda p: (0, 0), pipeline_mode=pl.Buffered(1))
    return pl.pallas_call(
        functools.partial(ramp_kernel, total=total),
        out_shape=jax.ShapeDtypeStruct(shape, jnp.float32),
        grid=(views // step,),
        in_specs=[pl.BlockSpec((blocks, rows, step, width), lambda p: (0, 0, p, 0)), band, band]
        + [pl.BlockSpec((ref.shape[0], step, STITCH), lambda p: (0, p, 0)) for ref in done],
        out_specs=out_spec,
        compiler_params=pltpu.CompilerParams(vmem_limit_bytes=RAMP_VMEM),
        cost_estimate=pl.CostEstimate(
            flops=3 * 2 * rows * views * STITCH * 1536,
            bytes_accessed=8 * rows * views * STITCH + 4 * high.size,
            transcendentals=0,
        ),
        name="ramp",
    )(x, high, low, *done)


def shards(
    raw_counts,
    dark_frames,
    flat_frames,
    dark_index,
    flat_index,
    center_offset,
    blend_width,
    stripe_gain,
    ramp_window,
):
    devices = lax.axis_size("ang")
    half = devices // 2
    rows = raw_counts.shape[1]
    upper = lax.axis_index("ang") >= half
    offset = center_offset[0]
    spread = blend_width[0].astype(jnp.float32)

    as_lines = lambda frames: (
        frames.reshape(-1, rows, DET // 128, 128).transpose(0, 2, 1, 3).reshape(-1, rows * DET // 128, 128)
    )
    raw = as_lines(raw_counts).reshape(-1, 128)
    dark, flat = as_lines(dark_frames), as_lines(flat_frames)
    indices = (dark_index, flat_index)

    place = jnp.arange(DET, dtype=jnp.int32)
    first_low = jnp.where(upper, offset + 1, DET - offset)
    position = jnp.where(place >= first_low, place, place + DET).astype(jnp.float32)
    weight = jnp.clip((position - DET + 0.5 * spread) / spread, 0.0, 1.0)
    weight = jnp.where(upper, 1.0 - weight, weight)[None, :]
    scalars = jnp.stack([upper.astype(jnp.int32), first_low.astype(jnp.int32)])

    frequency = jnp.arange(DET + 1).astype(jnp.float32)
    stripe_line = ring_lines(impulse(stripe_gain, VIEWS))
    ramp_line = ring_lines(impulse(4.0 * frequency / STITCH * ramp_window, STITCH))
    stripe_high, stripe_low = bands(stripe_line, False)
    ramp_high, ramp_low = bands(ramp_line, True)

    groups = [list(range(half)), list(range(half, devices))]
    chunk = rows // CHUNKS
    done = []
    for start in range(0, rows, chunk):
        sent = prepare(scalars, indices, raw, dark, flat, weight, start, chunk, half)
        columns = lax.all_to_all(sent, "ang", 0, 0, axis_index_groups=groups, tiled=True)
        destriped = destripe(columns, stripe_high, stripe_low, devices)
        view_rows = lax.all_to_all(destriped, "ang", 0, 0, tiled=True)
        if start + chunk < rows:
            done.append(ramp(view_rows, ramp_high, ramp_low))
    lines = ramp(view_rows, ramp_high, ramp_low, done, rows)
    views = VIEWS // devices
    filtered = lines.reshape(views, STITCH // 128, rows, 128).transpose(0, 2, 1, 3)
    return filtered.reshape(views, rows, STITCH)


def solution(mesh):
    in_specs = (
        P("ang", "slab", None),
        P(None, "slab", None),
        P(None, "slab", None),
        P("ang"),
        P("ang"),
        P(),
        P(),
        P(),
        P(),
    )
    out_specs = P("ang", "slab", None)
    return jax.shard_map(shards, mesh=mesh, in_specs=in_specs, out_specs=out_specs, check_vma=False)
```

```python
import functools

import jax
import jax.numpy as jnp
import numpy as np
from jax import lax
from jax.experimental import pallas as pl
from jax.experimental.pallas import tpu as pltpu
from jax.sharding import PartitionSpec as P

DET = 2048
VIEWS = 2048
STITCH = 2 * DET
EDGE = 64
TILE = 256
CHUNKS = [2, 2]
HELD = 5
KEPT = 3
CROSS = True
STEP = 128
UNROLL = 4
STRIPE_UNROLL = 2
RAMP_UNROLL = 4
MIB = 1024 * 1024
RAMP_VMEM = 36 * MIB
STRIPE_VMEM = 40 * MIB
PREPARE_VMEM = 56 * MIB

precise = lax.Precision.HIGHEST


def impulse(gains, length):
    inner = 64
    period = length // inner
    outer = period // 2
    phase = lambda rows, cols, whole: 2.0 * np.pi * (np.outer(rows, cols) % whole) / whole
    first = phase(np.arange(period), np.arange(outer), period)
    turn = phase(np.arange(period), np.arange(inner), length)
    last = phase(np.arange(inner), np.arange(inner), inner)
    table = lambda values: jnp.asarray(values.astype(np.float32))
    doubled = np.full((length // 2,), 2.0 / length, np.float32)
    doubled[0] = 1.0 / length
    coefs = (gains[:-1] * doubled).reshape(outer, inner)
    real = jnp.dot(table(np.cos(first)), coefs, precision=precise)
    imag = jnp.dot(table(np.sin(first)), coefs, precision=precise)
    cos_turn, sin_turn = table(np.cos(turn)), table(np.sin(turn))
    turned_real = real * cos_turn - imag * sin_turn
    turned_imag = real * sin_turn + imag * cos_turn
    contract = (((1,), (1,)), ((), ()))
    line = lax.dot_general(table(np.cos(last)), turned_real, contract, precision=precise)
    line = line - lax.dot_general(table(np.sin(last)), turned_imag, contract, precision=precise)
    signs = table(np.where(np.arange(period) % 2 == 0, 1.0, -1.0) / length)
    return (line + signs[None, :] * gains[-1]).reshape(length)


def ring_lines(line):
    quarter = line.shape[0] // 4
    q = line.reshape(4, quarter)
    even, odd = q[0] + q[2], q[1] + q[3]
    cyclic = 0.25 * (even + odd)
    negative = 0.25 * (even - odd)
    wide = 0.5 * jnp.concatenate([q[0] - q[2], q[1] - q[3]])
    return jnp.concatenate([cyclic, cyclic, negative, -negative, wide, -wide])[None, :]


def ring_spans(quarter):
    return ((0, quarter), (2 * quarter, quarter), (4 * quarter, 2 * quarter))


def band_kernel(line_ref, high_ref, low_ref, *, flip):
    quarter = line_ref.shape[1] // 8
    step = TILE if flip else 32
    for start, size in ring_spans(quarter):
        row = line_ref[:, start : start + 2 * size]
        wide = jnp.broadcast_to(row, (step, 2 * size))
        for top in range(0, TILE, step):
            shifted = pltpu.roll(wide, size - TILE + top, 1, stride=1, stride_axis=0)
            if flip:
                shifted = shifted.T
            high = shifted.astype(jnp.bfloat16)
            low = (shifted - high.astype(jnp.float32)).astype(jnp.bfloat16)
            if flip:
                place = (slice(start, start + 2 * size), slice(None))
            else:
                place = (slice(top, top + step), slice(start, start + 2 * size))
            high_ref[place] = high
            low_ref[place] = low


def bands(line, flip):
    size = line.shape[1]
    shape = jax.ShapeDtypeStruct((size, TILE) if flip else (TILE, size), jnp.bfloat16)
    return pl.pallas_call(
        functools.partial(band_kernel, flip=flip),
        out_shape=(shape, shape),
        compiler_params=pltpu.CompilerParams(vmem_limit_bytes=40 * MIB),
        cost_estimate=pl.CostEstimate(
            flops=4 * TILE * size, bytes_accessed=4 * TILE * size, transcendentals=0
        ),
        name="bands",
    )(line)


def split(values):
    high = values.astype(jnp.bfloat16)
    return high, (values - high.astype(jnp.float32)).astype(jnp.bfloat16)


def dot32(left, right, contract):
    return lax.dot_general(left, right, (contract, ((), ())), preferred_element_type=jnp.float32)


def prepare_kernel(
    scalars, dark_index, flat_index, raw_ref, dark_ref, flat_ref, weight_ref, out_ref, turned_ref, *, start
):
    count, rows, share, width = out_ref.shape
    blocks = DET // 128
    lines = dark_ref.shape[1]
    total = lines // blocks
    group = 8 // total if total < 8 else 1
    upper, shift = scalars[0], scalars[1]
    turn, jump = shift % 128, shift // 128
    lane = lax.broadcasted_iota(jnp.int32, (share, 128), 1)
    back = (lane + (128 - turn)) & 127
    pick = jnp.where(upper != 0, 127 - back, back)
    first = pl.program_id(0) * share

    def logs(eight, carry):
        pieces = []
        for one in range(8):
            view = eight * 8 + one
            dark = dark_ref[dark_index[first + view]]
            flat = flat_ref[flat_index[first + view]]
            raw = raw_ref[pl.ds(pl.multiple_of(view * lines, 8), lines), :]
            pieces.append(jnp.log(flat - dark) - jnp.log(raw - dark))
        top = pl.ds(pl.multiple_of(eight * 8, 8), 8)
        stacked = jnp.stack(pieces)
        for part in range(blocks // group):
            square = stacked[:, part * group * total : (part + 1) * group * total]
            square = pltpu.einshape("abc->bac", square)
            for inner in range(group):
                for row in range(rows):
                    turned_ref[row, part * group + inner, top, :] = square[inner * total + start + row]
        return carry

    lax.fori_loop(0, share // 8, logs, 0)

    def turned(block):
        source = jnp.where(upper != 0, blocks - 1 - block, block)
        return [jnp.take_along_axis(turned_ref[row, source], pick, axis=1) for row in range(rows)]

    def body(block, before):
        now = turned(block)
        target = (block + jump) % blocks
        place = pl.ds(pl.multiple_of(target * 128, 128), 128)
        weight = weight_ref[:, place]
        for row in range(rows):
            mixed = jnp.where(lane >= turn, now[row], before[row]) * weight
            if width >= 128:
                per = width // 128
                inside = pl.ds(pl.multiple_of((target % per) * 128, 128), 128)
                out_ref[target // per, row, :, inside] = mixed
            else:
                per = 128 // width
                for part in range(per):
                    out_ref[target * per + part, row] = mixed[:, part * width : (part + 1) * width]
        return now

    lax.fori_loop(0, blocks, body, turned(blocks - 1), unroll=UNROLL)


def prepare(scalars, indices, raw, dark, flat, weight, start, rows, count):
    share = indices[0].shape[0]
    width = DET // count
    step = min(share, STEP)
    lines = raw.shape[0] // share
    return pl.pallas_call(
        functools.partial(prepare_kernel, start=start),
        out_shape=jax.ShapeDtypeStruct((count, rows, share, width), jnp.float32),
        grid_spec=pltpu.PrefetchScalarGridSpec(
            num_scalar_prefetch=3,
            grid=(share // step,),
            in_specs=[
                pl.BlockSpec((lines * step, 128), lambda p, *s: (p, 0)),
                pl.BlockSpec(dark.shape, lambda p, *s: (0, 0, 0)),
                pl.BlockSpec(flat.shape, lambda p, *s: (0, 0, 0)),
                pl.BlockSpec((1, DET), lambda p, *s: (0, 0)),
            ],
            out_specs=pl.BlockSpec((count, rows, step, width), lambda p, *s: (0, 0, p, 0)),
            scratch_shapes=[pltpu.VMEM((rows, DET // 128, step, 128), jnp.float32)],
        ),
        compiler_params=pltpu.CompilerParams(vmem_limit_bytes=PREPARE_VMEM),
        cost_estimate=pl.CostEstimate(
            flops=20 * rows * share * DET,
            bytes_accessed=4 * rows * share * DET + 4 * raw.size,
            transcendentals=2 * raw.size,
        ),
        name="prepare",
    )(scalars, *indices, raw, dark, flat, weight)


def band_place(start, size, block):
    return pl.ds(pl.multiple_of(start + size - TILE - TILE * block, TILE), size)


def destripe_kernel(scalars, x_ref, high_ref, low_ref, *refs):
    *out_refs, full_ref = refs
    width = x_ref.shape[3]
    quarter = VIEWS // 4
    x = x_ref[...].reshape(4, quarter, width)
    even, odd = x[0] + x[2], x[1] + x[3]
    wide = jnp.concatenate([x[0] - x[2], x[1] - x[3]], axis=0)
    rings = [split(ring) for ring in (even + odd, even - odd, wide)]
    spans = ring_spans(quarter)

    def product(ring, block):
        place = band_place(*spans[ring], block)
        high, low = high_ref[:, place], low_ref[:, place]
        ring_high, ring_low = rings[ring]
        piece = dot32(high, ring_high, ((1,), (0,)))
        piece += dot32(high, ring_low, ((1,), (0,)))
        return piece + dot32(low, ring_high, ((1,), (0,)))

    count = quarter // TILE

    def body(block, carry):
        cyclic, negative = product(0, block), product(1, block)
        for part, both in enumerate((cyclic + negative, cyclic - negative)):
            wide = product(2, block + part * count)
            top = pl.multiple_of(part * quarter + block * TILE, TILE)
            full_ref[pl.ds(top, TILE), :] = both + wide
            full_ref[pl.ds(top + 2 * quarter, TILE), :] = both - wide
        return carry

    lax.fori_loop(0, count, body, 0, unroll=STRIPE_UNROLL)
    if len(out_refs) == 1:
        out_refs[0][...] = full_ref[...].reshape(out_refs[0].shape)
        return
    half = len(out_refs) // 2
    views = out_refs[0].shape[1]
    upper, me = scalars[0], scalars[1]
    for place, out_ref in enumerate(out_refs):
        side = upper if place < half else 1 - upper
        owner = side * half + (me ^ place % half)
        out_ref[0] = full_ref[pl.ds(pl.multiple_of(owner * views, views), views), :]


def destripe(scalars, x, high, low, devices, crossing):
    count, rows, share, width = x.shape
    views = VIEWS // devices
    if crossing:
        shapes = [jax.ShapeDtypeStruct((rows, views, width), jnp.float32)] * devices
        out_specs = [pl.BlockSpec((1, views, width), lambda r, s: (r, 0, 0))] * devices
    else:
        shapes = [jax.ShapeDtypeStruct((devices, rows, views, width), jnp.float32)]
        out_specs = [pl.BlockSpec((devices, 1, views, width), lambda r, s: (0, r, 0, 0))]
    band = pl.BlockSpec(high.shape, lambda r, s: (0, 0), pipeline_mode=pl.Buffered(1))
    return pl.pallas_call(
        destripe_kernel,
        out_shape=shapes,
        grid_spec=pltpu.PrefetchScalarGridSpec(
            num_scalar_prefetch=1,
            grid=(rows,),
            in_specs=[pl.BlockSpec((count, 1, share, width), lambda r, s: (0, r, 0, 0)), band, band],
            out_specs=out_specs,
            scratch_shapes=[pltpu.VMEM((VIEWS, width), jnp.float32)],
        ),
        compiler_params=pltpu.CompilerParams(vmem_limit_bytes=STRIPE_VMEM),
        cost_estimate=pl.CostEstimate(
            flops=3 * 2 * rows * width * VIEWS * 768,
            bytes_accessed=8 * rows * VIEWS * width + 4 * high.size,
            transcendentals=0,
        ),
        name="destripe",
    )(scalars, x, high, low)


def ramp_kernel(scalars, *refs, total, parts):
    part_refs, refs = refs[:parts], refs[parts:]
    high_ref, low_ref, *done_refs, y_ref, full_ref = refs
    rows, views, width = part_refs[0].shape[-3:]
    depth = rows * views
    upper, me = scalars[0], scalars[1]
    half = DET // width
    if parts > 1:
        for turn, part_ref in enumerate(part_refs):
            place = pl.ds(pl.multiple_of((me ^ turn % half) * width, 128), width)
            full_ref[turn // half, :, place] = part_ref[...].reshape(depth, width)
        own, other = full_ref[0], full_ref[1]
    else:
        pieces = [part_refs[0][block].reshape(depth, width) for block in range(2 * half)]
        own = jnp.concatenate(pieces[:half], axis=1)
        other = jnp.concatenate(pieces[half:], axis=1)
    place = lax.broadcasted_iota(jnp.int32, (1, DET), 1)
    direct_sign = jnp.where(place >= DET - EDGE, 1.0, -1.0)
    partner_sign = jnp.where(place < EDGE, -1.0, 1.0)
    own_sign = jnp.where(upper != 0, partner_sign, direct_sign)
    other_sign = jnp.where(upper != 0, direct_sign, partner_sign)
    added = own + other
    wide = own * own_sign + other * other_sign
    quarter = DET // 2
    left_half, right_half = added[:, :quarter], added[:, quarter:]
    rings = [split(ring) for ring in (left_half + right_half, left_half - right_half, wide)]
    spans = ring_spans(quarter)

    def product(ring, block):
        place = band_place(*spans[ring], block)
        high, low = high_ref[place, :], low_ref[place, :]
        ring_high, ring_low = rings[ring]
        piece = dot32(ring_high, high, ((1,), (0,)))
        piece += dot32(ring_low, high, ((1,), (0,)))
        return piece + dot32(ring_high, low, ((1,), (0,)))

    def emit(left, values):
        place = pl.ds(pl.multiple_of(left, TILE), TILE)
        values = values.reshape(rows, views, TILE)
        if not total:
            y_ref[:, :, place] = values
            return
        lines = [ref[row, :, place] for ref in done_refs for row in range(ref.shape[0])]
        lines += [values[row] for row in range(rows)]
        parts = TILE // 128
        square = jnp.stack([line[:, part * 128 : (part + 1) * 128] for part in range(parts) for line in lines])
        place = pl.ds(pl.multiple_of(left // 128 * total, parts * total), parts * total)
        y_ref[:, place, :] = pltpu.einshape("abc->bac", square)

    count = quarter // TILE

    def body(block, carry):
        cyclic, negative = product(0, block), product(1, block)
        for part, both in enumerate((cyclic + negative, cyclic - negative)):
            wide = product(2, block + part * count)
            left = part * quarter + block * TILE
            emit(left, both + wide)
            emit(left + DET, both - wide)
        return carry

    lax.fori_loop(0, count, body, 0, unroll=RAMP_UNROLL)


def ramp(scalars, parts, high, low, done=(), total=0):
    rows, views, width = parts[0].shape[-3:]
    step = min(views, max(128 // pl.next_power_of_2(rows), 8))
    if total:
        shape = (views, STITCH // 128 * total, 128)
        out_spec = pl.BlockSpec((step,) + shape[1:], lambda p, s: (p, 0, 0))
    else:
        shape = (rows, views, STITCH)
        out_spec = pl.BlockSpec((rows, step, STITCH), lambda p, s: (0, p, 0))
    band = pl.BlockSpec(high.shape, lambda p, s: (0, 0), pipeline_mode=pl.Buffered(1))
    middle = lambda ref: pl.BlockSpec(
        ref.shape[:-2] + (step, ref.shape[-1]), lambda p, s: (0,) * (ref.ndim - 2) + (p, 0)
    )
    return pl.pallas_call(
        functools.partial(ramp_kernel, total=total, parts=len(parts)),
        out_shape=jax.ShapeDtypeStruct(shape, jnp.float32),
        grid_spec=pltpu.PrefetchScalarGridSpec(
            num_scalar_prefetch=1,
            grid=(views // step,),
            in_specs=[middle(ref) for ref in parts] + [band, band] + [middle(ref) for ref in done],
            out_specs=out_spec,
            scratch_shapes=[pltpu.VMEM((2, rows * step, DET), jnp.float32)],
        ),
        compiler_params=pltpu.CompilerParams(vmem_limit_bytes=RAMP_VMEM),
        cost_estimate=pl.CostEstimate(
            flops=3 * 2 * rows * views * STITCH * 1536,
            bytes_accessed=8 * rows * views * STITCH + 4 * high.size,
            transcendentals=0,
        ),
        name="ramp",
    )(scalars, *parts, high, low, *done)


def shards(
    raw_counts,
    dark_frames,
    flat_frames,
    dark_index,
    flat_index,
    center_offset,
    blend_width,
    stripe_gain,
    ramp_window,
):
    devices = lax.axis_size("ang")
    half = devices // 2
    rows = raw_counts.shape[1]
    upper = lax.axis_index("ang") >= half
    offset = center_offset[0]
    spread = blend_width[0].astype(jnp.float32)

    as_lines = lambda frames: (
        frames.reshape(-1, rows, DET // 128, 128).transpose(0, 2, 1, 3).reshape(-1, rows * DET // 128, 128)
    )
    raw = as_lines(raw_counts).reshape(-1, 128)
    dark, flat = as_lines(dark_frames), as_lines(flat_frames)
    indices = (dark_index, flat_index)

    place = jnp.arange(DET, dtype=jnp.int32)
    first_low = jnp.where(upper, offset + 1, DET - offset)
    position = jnp.where(place >= first_low, place, place + DET).astype(jnp.float32)
    weight = jnp.clip((position - DET + 0.5 * spread) / spread, 0.0, 1.0)
    weight = jnp.where(upper, 1.0 - weight, weight)[None, :]
    scalars = jnp.stack([upper.astype(jnp.int32), first_low.astype(jnp.int32)])

    frequency = jnp.arange(DET + 1).astype(jnp.float32)
    stripe_line = ring_lines(impulse(stripe_gain, VIEWS))
    ramp_line = ring_lines(impulse(4.0 * frequency / STITCH * ramp_window, STITCH))
    stripe_high, stripe_low = bands(stripe_line, False)
    ramp_high, ramp_low = bands(ramp_line, True)

    groups = [list(range(half)), list(range(half, devices))]
    crossing = CROSS and DET // half >= 128
    sides = jnp.stack([upper.astype(jnp.int32), lax.axis_index("ang") % half])
    sides = sides if crossing else jnp.zeros_like(sides)

    def deliver(part, place):
        flip, turn = place // half, place % half
        if place == 0:
            return part
        pairs = [(src, (src // half ^ flip) * half + (src % half ^ turn)) for src in range(devices)]
        return lax.ppermute(part, "ang", pairs)

    sizes = CHUNKS if sum(CHUNKS) == rows else [rows]
    starts = [sum(sizes[:i]) for i in range(len(sizes))]
    fresh, crossed, parts = [], [], []
    for i, (start, size) in enumerate(zip(starts, sizes)):
        sent = prepare(scalars, indices, raw, dark, flat, weight, start, size, half)
        if i == 1:
            sent, stripe_high, stripe_low = lax.optimization_barrier((sent, stripe_high, stripe_low))
        columns = lax.all_to_all(sent, "ang", 0, 0, axis_index_groups=groups, tiled=True)
        if crossing and i >= 1:
            columns, crossed[i - 1][:HELD] = lax.optimization_barrier((columns, crossed[i - 1][:HELD]))
        fresh.append(destripe(sides, columns, stripe_high, stripe_low, devices, crossing))
        if crossing:
            crossed.append([deliver(part, half + place) for place, part in enumerate(fresh[i][half:])])
    for i, pieces in enumerate(fresh):
        if not crossing:
            parts.append([lax.all_to_all(pieces[0], "ang", 0, 0, tiled=True)])
            continue
        own = pieces[:half]
        if i + 1 < len(sizes) and KEPT > 0:
            own, crossed[i + 1][:KEPT] = lax.optimization_barrier((own, crossed[i + 1][:KEPT]))
        elif i + 1 < len(sizes):
            own, _ = lax.optimization_barrier((own, fresh[i + 1][0]))
        parts.append([deliver(part, place) for place, part in enumerate(own)] + crossed[i])
    done = []
    for pieces in parts[:-1]:
        done.append(ramp(sides, pieces, ramp_high, ramp_low))
    lines = ramp(sides, parts[-1], ramp_high, ramp_low, done, rows)
    views = VIEWS // devices
    filtered = lines.reshape(views, STITCH // 128, rows, 128).transpose(0, 2, 1, 3)
    return filtered.reshape(views, rows, STITCH)


def solution(mesh):
    in_specs = (
        P("ang", "slab", None),
        P(None, "slab", None),
        P(None, "slab", None),
        P("ang"),
        P("ang"),
        P(),
        P(),
        P(),
        P(),
    )
    out_specs = P("ang", "slab", None)
    return jax.shard_map(shards, mesh=mesh, in_specs=in_specs, out_specs=out_specs, check_vma=False)
```

```python
import functools

import jax
import jax.numpy as jnp
import numpy as np
from jax import lax
from jax.experimental import pallas as pl
from jax.experimental.pallas import tpu as pltpu
from jax.sharding import PartitionSpec as P

DET = 2048
VIEWS = 2048
STITCH = 2 * DET
EDGE = 64
TILE = 256
CHUNKS = [2, 2]
HELD = 4
KEPT = 2
CROSS = True
STEP = 128
UNROLL = 4
STRIPE_UNROLL = 2
RAMP_UNROLL = 4
MIB = 1024 * 1024
RAMP_VMEM = 36 * MIB
STRIPE_VMEM = 40 * MIB
PREPARE_VMEM = 56 * MIB

precise = lax.Precision.HIGHEST


def impulse(gains, length):
    inner = 64
    period = length // inner
    outer = period // 2
    phase = lambda rows, cols, whole: 2.0 * np.pi * (np.outer(rows, cols) % whole) / whole
    first = phase(np.arange(period), np.arange(outer), period)
    turn = phase(np.arange(period), np.arange(inner), length)
    last = phase(np.arange(inner), np.arange(inner), inner)
    table = lambda values: jnp.asarray(values.astype(np.float32))
    doubled = np.full((length // 2,), 2.0 / length, np.float32)
    doubled[0] = 1.0 / length
    coefs = (gains[:-1] * doubled).reshape(outer, inner)
    real = jnp.dot(table(np.cos(first)), coefs, precision=precise)
    imag = jnp.dot(table(np.sin(first)), coefs, precision=precise)
    cos_turn, sin_turn = table(np.cos(turn)), table(np.sin(turn))
    turned_real = real * cos_turn - imag * sin_turn
    turned_imag = real * sin_turn + imag * cos_turn
    contract = (((1,), (1,)), ((), ()))
    line = lax.dot_general(table(np.cos(last)), turned_real, contract, precision=precise)
    line = line - lax.dot_general(table(np.sin(last)), turned_imag, contract, precision=precise)
    signs = table(np.where(np.arange(period) % 2 == 0, 1.0, -1.0) / length)
    return (line + signs[None, :] * gains[-1]).reshape(length)


def ring_lines(line):
    quarter = line.shape[0] // 4
    q = line.reshape(4, quarter)
    even, odd = q[0] + q[2], q[1] + q[3]
    cyclic = 0.25 * (even + odd)
    negative = 0.25 * (even - odd)
    wide = 0.5 * jnp.concatenate([q[0] - q[2], q[1] - q[3]])
    return jnp.concatenate([cyclic, cyclic, negative, -negative, wide, -wide])[None, :]


def ring_spans(quarter):
    return ((0, quarter), (2 * quarter, quarter), (4 * quarter, 2 * quarter))


def band_kernel(line_ref, high_ref, low_ref, *, flip):
    quarter = line_ref.shape[1] // 8
    step = TILE if flip else 32
    for start, size in ring_spans(quarter):
        row = line_ref[:, start : start + 2 * size]
        wide = jnp.broadcast_to(row, (step, 2 * size))
        for top in range(0, TILE, step):
            shifted = pltpu.roll(wide, size - TILE + top, 1, stride=1, stride_axis=0)
            if flip:
                shifted = shifted.T
            high = shifted.astype(jnp.bfloat16)
            low = (shifted - high.astype(jnp.float32)).astype(jnp.bfloat16)
            if flip:
                place = (slice(start, start + 2 * size), slice(None))
            else:
                place = (slice(top, top + step), slice(start, start + 2 * size))
            high_ref[place] = high
            low_ref[place] = low


def bands(line, flip):
    size = line.shape[1]
    shape = jax.ShapeDtypeStruct((size, TILE) if flip else (TILE, size), jnp.bfloat16)
    return pl.pallas_call(
        functools.partial(band_kernel, flip=flip),
        out_shape=(shape, shape),
        compiler_params=pltpu.CompilerParams(vmem_limit_bytes=40 * MIB),
        cost_estimate=pl.CostEstimate(
            flops=4 * TILE * size, bytes_accessed=4 * TILE * size, transcendentals=0
        ),
        name="bands",
    )(line)


def split(values):
    high = values.astype(jnp.bfloat16)
    return high, (values - high.astype(jnp.float32)).astype(jnp.bfloat16)


def dot32(left, right, contract):
    return lax.dot_general(left, right, (contract, ((), ())), preferred_element_type=jnp.float32)


def prepare_kernel(
    scalars, dark_index, flat_index, raw_ref, dark_ref, flat_ref, weight_ref, out_ref, turned_ref, *, start
):
    count, rows, share, width = out_ref.shape
    blocks = DET // 128
    lines = dark_ref.shape[1]
    total = lines // blocks
    group = 8 // total if total < 8 else 1
    upper, shift = scalars[0], scalars[1]
    turn, jump = shift % 128, shift // 128
    lane = lax.broadcasted_iota(jnp.int32, (share, 128), 1)
    back = (lane + (128 - turn)) & 127
    pick = jnp.where(upper != 0, 127 - back, back)
    first = pl.program_id(0) * share

    def logs(eight, carry):
        pieces = []
        for one in range(8):
            view = eight * 8 + one
            dark = dark_ref[dark_index[first + view]]
            flat = flat_ref[flat_index[first + view]]
            raw = raw_ref[pl.ds(pl.multiple_of(view * lines, 8), lines), :]
            pieces.append(jnp.log(flat - dark) - jnp.log(raw - dark))
        top = pl.ds(pl.multiple_of(eight * 8, 8), 8)
        stacked = jnp.stack(pieces)
        for part in range(blocks // group):
            square = stacked[:, part * group * total : (part + 1) * group * total]
            square = pltpu.einshape("abc->bac", square)
            for inner in range(group):
                for row in range(rows):
                    turned_ref[row, part * group + inner, top, :] = square[inner * total + start + row]
        return carry

    lax.fori_loop(0, share // 8, logs, 0)

    def turned(block):
        source = jnp.where(upper != 0, blocks - 1 - block, block)
        return [jnp.take_along_axis(turned_ref[row, source], pick, axis=1) for row in range(rows)]

    def body(block, before):
        now = turned(block)
        target = (block + jump) % blocks
        place = pl.ds(pl.multiple_of(target * 128, 128), 128)
        weight = weight_ref[:, place]
        for row in range(rows):
            mixed = jnp.where(lane >= turn, now[row], before[row]) * weight
            if width >= 128:
                per = width // 128
                inside = pl.ds(pl.multiple_of((target % per) * 128, 128), 128)
                out_ref[target // per, row, :, inside] = mixed
            else:
                per = 128 // width
                for part in range(per):
                    out_ref[target * per + part, row] = mixed[:, part * width : (part + 1) * width]
        return now

    lax.fori_loop(0, blocks, body, turned(blocks - 1), unroll=UNROLL)


def prepare(scalars, indices, raw, dark, flat, weight, start, rows, count):
    share = indices[0].shape[0]
    width = DET // count
    step = min(share, STEP)
    lines = raw.shape[0] // share
    return pl.pallas_call(
        functools.partial(prepare_kernel, start=start),
        out_shape=jax.ShapeDtypeStruct((count, rows, share, width), jnp.float32),
        grid_spec=pltpu.PrefetchScalarGridSpec(
            num_scalar_prefetch=3,
            grid=(share // step,),
            in_specs=[
                pl.BlockSpec((lines * step, 128), lambda p, *s: (p, 0)),
                pl.BlockSpec(dark.shape, lambda p, *s: (0, 0, 0)),
                pl.BlockSpec(flat.shape, lambda p, *s: (0, 0, 0)),
                pl.BlockSpec((1, DET), lambda p, *s: (0, 0)),
            ],
            out_specs=pl.BlockSpec((count, rows, step, width), lambda p, *s: (0, 0, p, 0)),
            scratch_shapes=[pltpu.VMEM((rows, DET // 128, step, 128), jnp.float32)],
        ),
        compiler_params=pltpu.CompilerParams(vmem_limit_bytes=PREPARE_VMEM),
        cost_estimate=pl.CostEstimate(
            flops=20 * rows * share * DET,
            bytes_accessed=4 * rows * share * DET + 4 * raw.size,
            transcendentals=2 * raw.size,
        ),
        name="prepare",
    )(scalars, *indices, raw, dark, flat, weight)


def band_place(start, size, block):
    return pl.ds(pl.multiple_of(start + size - TILE - TILE * block, TILE), size)


def destripe_kernel(scalars, x_ref, high_ref, low_ref, *refs):
    *out_refs, full_ref = refs
    width = x_ref.shape[3]
    quarter = VIEWS // 4
    x = x_ref[...].reshape(4, quarter, width)
    even, odd = x[0] + x[2], x[1] + x[3]
    wide = jnp.concatenate([x[0] - x[2], x[1] - x[3]], axis=0)
    rings = [split(ring) for ring in (even + odd, even - odd, wide)]
    spans = ring_spans(quarter)

    def product(ring, block):
        place = band_place(*spans[ring], block)
        high, low = high_ref[:, place], low_ref[:, place]
        ring_high, ring_low = rings[ring]
        piece = dot32(high, ring_high, ((1,), (0,)))
        piece += dot32(high, ring_low, ((1,), (0,)))
        return piece + dot32(low, ring_high, ((1,), (0,)))

    count = quarter // TILE

    def body(block, carry):
        cyclic, negative = product(0, block), product(1, block)
        for part, both in enumerate((cyclic + negative, cyclic - negative)):
            wide = product(2, block + part * count)
            top = pl.multiple_of(part * quarter + block * TILE, TILE)
            full_ref[pl.ds(top, TILE), :] = both + wide
            full_ref[pl.ds(top + 2 * quarter, TILE), :] = both - wide
        return carry

    lax.fori_loop(0, count, body, 0, unroll=STRIPE_UNROLL)
    if len(out_refs) == 1:
        out_refs[0][...] = full_ref[...].reshape(out_refs[0].shape)
        return
    half = len(out_refs) // 2
    views = out_refs[0].shape[1]
    upper, me = scalars[0], scalars[1]
    for place, out_ref in enumerate(out_refs):
        side = upper if place < half else 1 - upper
        owner = side * half + (me ^ place % half)
        out_ref[0] = full_ref[pl.ds(pl.multiple_of(owner * views, views), views), :]


def destripe(scalars, x, high, low, devices, crossing):
    count, rows, share, width = x.shape
    views = VIEWS // devices
    if crossing:
        shapes = [jax.ShapeDtypeStruct((rows, views, width), jnp.float32)] * devices
        out_specs = [pl.BlockSpec((1, views, width), lambda r, s: (r, 0, 0))] * devices
    else:
        shapes = [jax.ShapeDtypeStruct((devices, rows, views, width), jnp.float32)]
        out_specs = [pl.BlockSpec((devices, 1, views, width), lambda r, s: (0, r, 0, 0))]
    band = pl.BlockSpec(high.shape, lambda r, s: (0, 0), pipeline_mode=pl.Buffered(1))
    return pl.pallas_call(
        destripe_kernel,
        out_shape=shapes,
        grid_spec=pltpu.PrefetchScalarGridSpec(
            num_scalar_prefetch=1,
            grid=(rows,),
            in_specs=[pl.BlockSpec((count, 1, share, width), lambda r, s: (0, r, 0, 0)), band, band],
            out_specs=out_specs,
            scratch_shapes=[pltpu.VMEM((VIEWS, width), jnp.float32)],
        ),
        compiler_params=pltpu.CompilerParams(vmem_limit_bytes=STRIPE_VMEM),
        cost_estimate=pl.CostEstimate(
            flops=3 * 2 * rows * width * VIEWS * 768,
            bytes_accessed=8 * rows * VIEWS * width + 4 * high.size,
            transcendentals=0,
        ),
        name="destripe",
    )(scalars, x, high, low)


def ramp_kernel(scalars, *refs, total, parts):
    part_refs, refs = refs[:parts], refs[parts:]
    high_ref, low_ref, *done_refs, y_ref, full_ref = refs
    rows, views, width = part_refs[0].shape[-3:]
    depth = rows * views
    upper, me = scalars[0], scalars[1]
    half = DET // width
    if parts > 1:
        for turn, part_ref in enumerate(part_refs):
            place = pl.ds(pl.multiple_of((me ^ turn % half) * width, 128), width)
            full_ref[turn // half, :, place] = part_ref[...].reshape(depth, width)
        own, other = full_ref[0], full_ref[1]
    else:
        pieces = [part_refs[0][block].reshape(depth, width) for block in range(2 * half)]
        own = jnp.concatenate(pieces[:half], axis=1)
        other = jnp.concatenate(pieces[half:], axis=1)
    place = lax.broadcasted_iota(jnp.int32, (1, DET), 1)
    direct_sign = jnp.where(place >= DET - EDGE, 1.0, -1.0)
    partner_sign = jnp.where(place < EDGE, -1.0, 1.0)
    own_sign = jnp.where(upper != 0, partner_sign, direct_sign)
    other_sign = jnp.where(upper != 0, direct_sign, partner_sign)
    added = own + other
    wide = own * own_sign + other * other_sign
    quarter = DET // 2
    left_half, right_half = added[:, :quarter], added[:, quarter:]
    rings = [split(ring) for ring in (left_half + right_half, left_half - right_half, wide)]
    spans = ring_spans(quarter)

    def product(ring, block):
        place = band_place(*spans[ring], block)
        high, low = high_ref[place, :], low_ref[place, :]
        ring_high, ring_low = rings[ring]
        piece = dot32(ring_high, high, ((1,), (0,)))
        piece += dot32(ring_low, high, ((1,), (0,)))
        return piece + dot32(ring_high, low, ((1,), (0,)))

    def emit(left, values):
        place = pl.ds(pl.multiple_of(left, TILE), TILE)
        values = values.reshape(rows, views, TILE)
        if not total:
            y_ref[:, :, place] = values
            return
        lines = [ref[row, :, place] for ref in done_refs for row in range(ref.shape[0])]
        lines += [values[row] for row in range(rows)]
        parts = TILE // 128
        square = jnp.stack([line[:, part * 128 : (part + 1) * 128] for part in range(parts) for line in lines])
        place = pl.ds(pl.multiple_of(left // 128 * total, parts * total), parts * total)
        y_ref[:, place, :] = pltpu.einshape("abc->bac", square)

    count = quarter // TILE

    def body(block, carry):
        cyclic, negative = product(0, block), product(1, block)
        for part, both in enumerate((cyclic + negative, cyclic - negative)):
            wide = product(2, block + part * count)
            left = part * quarter + block * TILE
            emit(left, both + wide)
            emit(left + DET, both - wide)
        return carry

    lax.fori_loop(0, count, body, 0, unroll=RAMP_UNROLL)


def ramp(scalars, parts, high, low, done=(), total=0):
    rows, views, width = parts[0].shape[-3:]
    step = min(views, max(128 // pl.next_power_of_2(rows), 8))
    if total:
        shape = (views, STITCH // 128 * total, 128)
        out_spec = pl.BlockSpec((step,) + shape[1:], lambda p, s: (p, 0, 0))
    else:
        shape = (rows, views, STITCH)
        out_spec = pl.BlockSpec((rows, step, STITCH), lambda p, s: (0, p, 0))
    band = pl.BlockSpec(high.shape, lambda p, s: (0, 0), pipeline_mode=pl.Buffered(1))
    middle = lambda ref: pl.BlockSpec(
        ref.shape[:-2] + (step, ref.shape[-1]), lambda p, s: (0,) * (ref.ndim - 2) + (p, 0)
    )
    return pl.pallas_call(
        functools.partial(ramp_kernel, total=total, parts=len(parts)),
        out_shape=jax.ShapeDtypeStruct(shape, jnp.float32),
        grid_spec=pltpu.PrefetchScalarGridSpec(
            num_scalar_prefetch=1,
            grid=(views // step,),
            in_specs=[middle(ref) for ref in parts] + [band, band] + [middle(ref) for ref in done],
            out_specs=out_spec,
            scratch_shapes=[pltpu.VMEM((2, rows * step, DET), jnp.float32)],
        ),
        compiler_params=pltpu.CompilerParams(vmem_limit_bytes=RAMP_VMEM),
        cost_estimate=pl.CostEstimate(
            flops=3 * 2 * rows * views * STITCH * 1536,
            bytes_accessed=8 * rows * views * STITCH + 4 * high.size,
            transcendentals=0,
        ),
        name="ramp",
    )(scalars, *parts, high, low, *done)


def shards(
    raw_counts,
    dark_frames,
    flat_frames,
    dark_index,
    flat_index,
    center_offset,
    blend_width,
    stripe_gain,
    ramp_window,
):
    devices = lax.axis_size("ang")
    half = devices // 2
    rows = raw_counts.shape[1]
    upper = lax.axis_index("ang") >= half
    offset = center_offset[0]
    spread = blend_width[0].astype(jnp.float32)

    as_lines = lambda frames: (
        frames.reshape(-1, rows, DET // 128, 128).transpose(0, 2, 1, 3).reshape(-1, rows * DET // 128, 128)
    )
    raw = as_lines(raw_counts).reshape(-1, 128)
    dark, flat = as_lines(dark_frames), as_lines(flat_frames)
    indices = (dark_index, flat_index)

    place = jnp.arange(DET, dtype=jnp.int32)
    first_low = jnp.where(upper, offset + 1, DET - offset)
    position = jnp.where(place >= first_low, place, place + DET).astype(jnp.float32)
    weight = jnp.clip((position - DET + 0.5 * spread) / spread, 0.0, 1.0)
    weight = jnp.where(upper, 1.0 - weight, weight)[None, :]
    scalars = jnp.stack([upper.astype(jnp.int32), first_low.astype(jnp.int32)])

    frequency = jnp.arange(DET + 1).astype(jnp.float32)
    stripe_line = ring_lines(impulse(stripe_gain, VIEWS))
    ramp_line = ring_lines(impulse(4.0 * frequency / STITCH * ramp_window, STITCH))
    stripe_high, stripe_low = bands(stripe_line, False)
    ramp_high, ramp_low = bands(ramp_line, True)

    groups = [list(range(half)), list(range(half, devices))]
    crossing = CROSS and DET // half >= 128
    sides = jnp.stack([upper.astype(jnp.int32), lax.axis_index("ang") % half])
    sides = sides if crossing else jnp.zeros_like(sides)

    def deliver(part, place):
        flip, turn = place // half, place % half
        if place == 0:
            return part
        pairs = [(src, (src // half ^ flip) * half + (src % half ^ turn)) for src in range(devices)]
        return lax.ppermute(part, "ang", pairs)

    sizes = CHUNKS if sum(CHUNKS) == rows else [rows]
    starts = [sum(sizes[:i]) for i in range(len(sizes))]
    fresh, crossed, parts = [], [], []
    for i, (start, size) in enumerate(zip(starts, sizes)):
        sent = prepare(scalars, indices, raw, dark, flat, weight, start, size, half)
        if i == 1:
            sent, stripe_high, stripe_low = lax.optimization_barrier((sent, stripe_high, stripe_low))
        columns = lax.all_to_all(sent, "ang", 0, 0, axis_index_groups=groups, tiled=True)
        if crossing and i >= 1:
            columns, crossed[i - 1][:HELD] = lax.optimization_barrier((columns, crossed[i - 1][:HELD]))
        fresh.append(destripe(sides, columns, stripe_high, stripe_low, devices, crossing))
        if crossing:
            crossed.append([deliver(part, half + place) for place, part in enumerate(fresh[i][half:])])
    for i, pieces in enumerate(fresh):
        if not crossing:
            parts.append([lax.all_to_all(pieces[0], "ang", 0, 0, tiled=True)])
            continue
        own = pieces[:half]
        if i + 1 < len(sizes) and KEPT > 0:
            own, crossed[i + 1][:KEPT] = lax.optimization_barrier((own, crossed[i + 1][:KEPT]))
        elif i + 1 < len(sizes):
            own, _ = lax.optimization_barrier((own, fresh[i + 1][0]))
        parts.append([deliver(part, place) for place, part in enumerate(own)] + crossed[i])
    done = []
    for pieces in parts[:-1]:
        done.append(ramp(sides, pieces, ramp_high, ramp_low))
    lines = ramp(sides, parts[-1], ramp_high, ramp_low, done, rows)
    views = VIEWS // devices
    filtered = lines.reshape(views, STITCH // 128, rows, 128).transpose(0, 2, 1, 3)
    return filtered.reshape(views, rows, STITCH)


def solution(mesh):
    in_specs = (
        P("ang", "slab", None),
        P(None, "slab", None),
        P(None, "slab", None),
        P("ang"),
        P("ang"),
        P(),
        P(),
        P(),
        P(),
    )
    out_specs = P("ang", "slab", None)
    return jax.shard_map(shards, mesh=mesh, in_specs=in_specs, out_specs=out_specs, check_vma=False)
```

```python
import functools

import jax
import jax.numpy as jnp
import numpy as np
from jax import lax
from jax.experimental import pallas as pl
from jax.experimental.pallas import tpu as pltpu
from jax.sharding import PartitionSpec as P

DET = 2048
VIEWS = 2048
STITCH = 2 * DET
EDGE = 64
TILE = 256
CHUNKS = [2, 2]
HELD = 4
KEPT = 1
CROSS = True
STEP = 128
UNROLL = 4
STRIPE_UNROLL = 2
RAMP_UNROLL = 4
MIB = 1024 * 1024
RAMP_VMEM = 36 * MIB
STRIPE_VMEM = 40 * MIB
PREPARE_VMEM = 56 * MIB

precise = lax.Precision.HIGHEST


def impulse(gains, length):
    inner = 64
    period = length // inner
    outer = period // 2
    phase = lambda rows, cols, whole: 2.0 * np.pi * (np.outer(rows, cols) % whole) / whole
    first = phase(np.arange(period), np.arange(outer), period)
    turn = phase(np.arange(period), np.arange(inner), length)
    last = phase(np.arange(inner), np.arange(inner), inner)
    table = lambda values: jnp.asarray(values.astype(np.float32))
    doubled = np.full((length // 2,), 2.0 / length, np.float32)
    doubled[0] = 1.0 / length
    coefs = (gains[:-1] * doubled).reshape(outer, inner)
    real = jnp.dot(table(np.cos(first)), coefs, precision=precise)
    imag = jnp.dot(table(np.sin(first)), coefs, precision=precise)
    cos_turn, sin_turn = table(np.cos(turn)), table(np.sin(turn))
    turned_real = real * cos_turn - imag * sin_turn
    turned_imag = real * sin_turn + imag * cos_turn
    contract = (((1,), (1,)), ((), ()))
    line = lax.dot_general(table(np.cos(last)), turned_real, contract, precision=precise)
    line = line - lax.dot_general(table(np.sin(last)), turned_imag, contract, precision=precise)
    signs = table(np.where(np.arange(period) % 2 == 0, 1.0, -1.0) / length)
    return (line + signs[None, :] * gains[-1]).reshape(length)


def ring_lines(line):
    quarter = line.shape[0] // 4
    q = line.reshape(4, quarter)
    even, odd = q[0] + q[2], q[1] + q[3]
    cyclic = 0.25 * (even + odd)
    negative = 0.25 * (even - odd)
    wide = 0.5 * jnp.concatenate([q[0] - q[2], q[1] - q[3]])
    return jnp.concatenate([cyclic, cyclic, negative, -negative, wide, -wide])[None, :]


def ring_spans(quarter):
    return ((0, quarter), (2 * quarter, quarter), (4 * quarter, 2 * quarter))


def band_kernel(line_ref, high_ref, low_ref, *, flip):
    quarter = line_ref.shape[1] // 8
    step = TILE if flip else 32
    for start, size in ring_spans(quarter):
        row = line_ref[:, start : start + 2 * size]
        wide = jnp.broadcast_to(row, (step, 2 * size))
        for top in range(0, TILE, step):
            shifted = pltpu.roll(wide, size - TILE + top, 1, stride=1, stride_axis=0)
            if flip:
                shifted = shifted.T
            high = shifted.astype(jnp.bfloat16)
            low = (shifted - high.astype(jnp.float32)).astype(jnp.bfloat16)
            if flip:
                place = (slice(start, start + 2 * size), slice(None))
            else:
                place = (slice(top, top + step), slice(start, start + 2 * size))
            high_ref[place] = high
            low_ref[place] = low


def bands(line, flip):
    size = line.shape[1]
    shape = jax.ShapeDtypeStruct((size, TILE) if flip else (TILE, size), jnp.bfloat16)
    return pl.pallas_call(
        functools.partial(band_kernel, flip=flip),
        out_shape=(shape, shape),
        compiler_params=pltpu.CompilerParams(vmem_limit_bytes=40 * MIB),
        cost_estimate=pl.CostEstimate(
            flops=4 * TILE * size, bytes_accessed=4 * TILE * size, transcendentals=0
        ),
        name="bands",
    )(line)


def split(values):
    high = values.astype(jnp.bfloat16)
    return high, (values - high.astype(jnp.float32)).astype(jnp.bfloat16)


def dot32(left, right, contract):
    return lax.dot_general(left, right, (contract, ((), ())), preferred_element_type=jnp.float32)


def prepare_kernel(
    scalars, dark_index, flat_index, raw_ref, dark_ref, flat_ref, weight_ref, out_ref, turned_ref, *, start
):
    count, rows, share, width = out_ref.shape
    blocks = DET // 128
    lines = dark_ref.shape[1]
    total = lines // blocks
    group = 8 // total if total < 8 else 1
    upper, shift = scalars[0], scalars[1]
    turn, jump = shift % 128, shift // 128
    lane = lax.broadcasted_iota(jnp.int32, (share, 128), 1)
    back = (lane + (128 - turn)) & 127
    pick = jnp.where(upper != 0, 127 - back, back)
    first = pl.program_id(0) * share

    def logs(eight, carry):
        pieces = []
        for one in range(8):
            view = eight * 8 + one
            dark = dark_ref[dark_index[first + view]]
            flat = flat_ref[flat_index[first + view]]
            raw = raw_ref[pl.ds(pl.multiple_of(view * lines, 8), lines), :]
            pieces.append(jnp.log(flat - dark) - jnp.log(raw - dark))
        top = pl.ds(pl.multiple_of(eight * 8, 8), 8)
        stacked = jnp.stack(pieces)
        for part in range(blocks // group):
            square = stacked[:, part * group * total : (part + 1) * group * total]
            square = pltpu.einshape("abc->bac", square)
            for inner in range(group):
                for row in range(rows):
                    turned_ref[row, part * group + inner, top, :] = square[inner * total + start + row]
        return carry

    lax.fori_loop(0, share // 8, logs, 0)

    def turned(block):
        source = jnp.where(upper != 0, blocks - 1 - block, block)
        return [jnp.take_along_axis(turned_ref[row, source], pick, axis=1) for row in range(rows)]

    def body(block, before):
        now = turned(block)
        target = (block + jump) % blocks
        place = pl.ds(pl.multiple_of(target * 128, 128), 128)
        weight = weight_ref[:, place]
        for row in range(rows):
            mixed = jnp.where(lane >= turn, now[row], before[row]) * weight
            if width >= 128:
                per = width // 128
                inside = pl.ds(pl.multiple_of((target % per) * 128, 128), 128)
                out_ref[target // per, row, :, inside] = mixed
            else:
                per = 128 // width
                for part in range(per):
                    out_ref[target * per + part, row] = mixed[:, part * width : (part + 1) * width]
        return now

    lax.fori_loop(0, blocks, body, turned(blocks - 1), unroll=UNROLL)


def prepare(scalars, indices, raw, dark, flat, weight, start, rows, count):
    share = indices[0].shape[0]
    width = DET // count
    step = min(share, STEP)
    lines = raw.shape[0] // share
    return pl.pallas_call(
        functools.partial(prepare_kernel, start=start),
        out_shape=jax.ShapeDtypeStruct((count, rows, share, width), jnp.float32),
        grid_spec=pltpu.PrefetchScalarGridSpec(
            num_scalar_prefetch=3,
            grid=(share // step,),
            in_specs=[
                pl.BlockSpec((lines * step, 128), lambda p, *s: (p, 0)),
                pl.BlockSpec(dark.shape, lambda p, *s: (0, 0, 0)),
                pl.BlockSpec(flat.shape, lambda p, *s: (0, 0, 0)),
                pl.BlockSpec((1, DET), lambda p, *s: (0, 0)),
            ],
            out_specs=pl.BlockSpec((count, rows, step, width), lambda p, *s: (0, 0, p, 0)),
            scratch_shapes=[pltpu.VMEM((rows, DET // 128, step, 128), jnp.float32)],
        ),
        compiler_params=pltpu.CompilerParams(vmem_limit_bytes=PREPARE_VMEM),
        cost_estimate=pl.CostEstimate(
            flops=20 * rows * share * DET,
            bytes_accessed=4 * rows * share * DET + 4 * raw.size,
            transcendentals=2 * raw.size,
        ),
        name="prepare",
    )(scalars, *indices, raw, dark, flat, weight)


def band_place(start, size, block):
    return pl.ds(pl.multiple_of(start + size - TILE - TILE * block, TILE), size)


def destripe_kernel(scalars, x_ref, high_ref, low_ref, *refs):
    *out_refs, full_ref = refs
    width = x_ref.shape[3]
    quarter = VIEWS // 4
    x = x_ref[...].reshape(4, quarter, width)
    even, odd = x[0] + x[2], x[1] + x[3]
    wide = jnp.concatenate([x[0] - x[2], x[1] - x[3]], axis=0)
    rings = [split(ring) for ring in (even + odd, even - odd, wide)]
    spans = ring_spans(quarter)

    def product(ring, block):
        place = band_place(*spans[ring], block)
        high, low = high_ref[:, place], low_ref[:, place]
        ring_high, ring_low = rings[ring]
        piece = dot32(high, ring_high, ((1,), (0,)))
        piece += dot32(high, ring_low, ((1,), (0,)))
        return piece + dot32(low, ring_high, ((1,), (0,)))

    count = quarter // TILE

    def body(block, carry):
        cyclic, negative = product(0, block), product(1, block)
        for part, both in enumerate((cyclic + negative, cyclic - negative)):
            wide = product(2, block + part * count)
            top = pl.multiple_of(part * quarter + block * TILE, TILE)
            full_ref[pl.ds(top, TILE), :] = both + wide
            full_ref[pl.ds(top + 2 * quarter, TILE), :] = both - wide
        return carry

    lax.fori_loop(0, count, body, 0, unroll=STRIPE_UNROLL)
    if len(out_refs) == 1:
        out_refs[0][...] = full_ref[...].reshape(out_refs[0].shape)
        return
    half = len(out_refs) // 2
    views = out_refs[0].shape[1]
    upper, me = scalars[0], scalars[1]
    for place, out_ref in enumerate(out_refs):
        side = upper if place < half else 1 - upper
        owner = side * half + (me ^ place % half)
        out_ref[0] = full_ref[pl.ds(pl.multiple_of(owner * views, views), views), :]


def destripe(scalars, x, high, low, devices, crossing):
    count, rows, share, width = x.shape
    views = VIEWS // devices
    if crossing:
        shapes = [jax.ShapeDtypeStruct((rows, views, width), jnp.float32)] * devices
        out_specs = [pl.BlockSpec((1, views, width), lambda r, s: (r, 0, 0))] * devices
    else:
        shapes = [jax.ShapeDtypeStruct((devices, rows, views, width), jnp.float32)]
        out_specs = [pl.BlockSpec((devices, 1, views, width), lambda r, s: (0, r, 0, 0))]
    band = pl.BlockSpec(high.shape, lambda r, s: (0, 0), pipeline_mode=pl.Buffered(1))
    return pl.pallas_call(
        destripe_kernel,
        out_shape=shapes,
        grid_spec=pltpu.PrefetchScalarGridSpec(
            num_scalar_prefetch=1,
            grid=(rows,),
            in_specs=[pl.BlockSpec((count, 1, share, width), lambda r, s: (0, r, 0, 0)), band, band],
            out_specs=out_specs,
            scratch_shapes=[pltpu.VMEM((VIEWS, width), jnp.float32)],
        ),
        compiler_params=pltpu.CompilerParams(vmem_limit_bytes=STRIPE_VMEM),
        cost_estimate=pl.CostEstimate(
            flops=3 * 2 * rows * width * VIEWS * 768,
            bytes_accessed=8 * rows * VIEWS * width + 4 * high.size,
            transcendentals=0,
        ),
        name="destripe",
    )(scalars, x, high, low)


def ramp_kernel(scalars, *refs, total, parts):
    part_refs, refs = refs[:parts], refs[parts:]
    high_ref, low_ref, *done_refs, y_ref, full_ref = refs
    rows, views, width = part_refs[0].shape[-3:]
    depth = rows * views
    upper, me = scalars[0], scalars[1]
    half = DET // width
    if parts > 1:
        for turn, part_ref in enumerate(part_refs):
            place = pl.ds(pl.multiple_of((me ^ turn % half) * width, 128), width)
            full_ref[turn // half, :, place] = part_ref[...].reshape(depth, width)
        own, other = full_ref[0], full_ref[1]
    else:
        pieces = [part_refs[0][block].reshape(depth, width) for block in range(2 * half)]
        own = jnp.concatenate(pieces[:half], axis=1)
        other = jnp.concatenate(pieces[half:], axis=1)
    place = lax.broadcasted_iota(jnp.int32, (1, DET), 1)
    direct_sign = jnp.where(place >= DET - EDGE, 1.0, -1.0)
    partner_sign = jnp.where(place < EDGE, -1.0, 1.0)
    own_sign = jnp.where(upper != 0, partner_sign, direct_sign)
    other_sign = jnp.where(upper != 0, direct_sign, partner_sign)
    added = own + other
    wide = own * own_sign + other * other_sign
    quarter = DET // 2
    left_half, right_half = added[:, :quarter], added[:, quarter:]
    rings = [split(ring) for ring in (left_half + right_half, left_half - right_half, wide)]
    spans = ring_spans(quarter)

    def product(ring, block):
        place = band_place(*spans[ring], block)
        high, low = high_ref[place, :], low_ref[place, :]
        ring_high, ring_low = rings[ring]
        piece = dot32(ring_high, high, ((1,), (0,)))
        piece += dot32(ring_low, high, ((1,), (0,)))
        return piece + dot32(ring_high, low, ((1,), (0,)))

    def emit(left, values):
        place = pl.ds(pl.multiple_of(left, TILE), TILE)
        values = values.reshape(rows, views, TILE)
        if not total:
            y_ref[:, :, place] = values
            return
        lines = [ref[row, :, place] for ref in done_refs for row in range(ref.shape[0])]
        lines += [values[row] for row in range(rows)]
        parts = TILE // 128
        square = jnp.stack([line[:, part * 128 : (part + 1) * 128] for part in range(parts) for line in lines])
        place = pl.ds(pl.multiple_of(left // 128 * total, parts * total), parts * total)
        y_ref[:, place, :] = pltpu.einshape("abc->bac", square)

    count = quarter // TILE

    def body(block, carry):
        cyclic, negative = product(0, block), product(1, block)
        for part, both in enumerate((cyclic + negative, cyclic - negative)):
            wide = product(2, block + part * count)
            left = part * quarter + block * TILE
            emit(left, both + wide)
            emit(left + DET, both - wide)
        return carry

    lax.fori_loop(0, count, body, 0, unroll=RAMP_UNROLL)


def ramp(scalars, parts, high, low, done=(), total=0):
    rows, views, width = parts[0].shape[-3:]
    step = min(views, max(128 // pl.next_power_of_2(rows), 8))
    if total:
        shape = (views, STITCH // 128 * total, 128)
        out_spec = pl.BlockSpec((step,) + shape[1:], lambda p, s: (p, 0, 0))
    else:
        shape = (rows, views, STITCH)
        out_spec = pl.BlockSpec((rows, step, STITCH), lambda p, s: (0, p, 0))
    band = pl.BlockSpec(high.shape, lambda p, s: (0, 0), pipeline_mode=pl.Buffered(1))
    middle = lambda ref: pl.BlockSpec(
        ref.shape[:-2] + (step, ref.shape[-1]), lambda p, s: (0,) * (ref.ndim - 2) + (p, 0)
    )
    return pl.pallas_call(
        functools.partial(ramp_kernel, total=total, parts=len(parts)),
        out_shape=jax.ShapeDtypeStruct(shape, jnp.float32),
        grid_spec=pltpu.PrefetchScalarGridSpec(
            num_scalar_prefetch=1,
            grid=(views // step,),
            in_specs=[middle(ref) for ref in parts] + [band, band] + [middle(ref) for ref in done],
            out_specs=out_spec,
            scratch_shapes=[pltpu.VMEM((2, rows * step, DET), jnp.float32)],
        ),
        compiler_params=pltpu.CompilerParams(vmem_limit_bytes=RAMP_VMEM),
        cost_estimate=pl.CostEstimate(
            flops=3 * 2 * rows * views * STITCH * 1536,
            bytes_accessed=8 * rows * views * STITCH + 4 * high.size,
            transcendentals=0,
        ),
        name="ramp",
    )(scalars, *parts, high, low, *done)


def shards(
    raw_counts,
    dark_frames,
    flat_frames,
    dark_index,
    flat_index,
    center_offset,
    blend_width,
    stripe_gain,
    ramp_window,
):
    devices = lax.axis_size("ang")
    half = devices // 2
    rows = raw_counts.shape[1]
    upper = lax.axis_index("ang") >= half
    offset = center_offset[0]
    spread = blend_width[0].astype(jnp.float32)

    as_lines = lambda frames: (
        frames.reshape(-1, rows, DET // 128, 128).transpose(0, 2, 1, 3).reshape(-1, rows * DET // 128, 128)
    )
    raw = as_lines(raw_counts).reshape(-1, 128)
    dark, flat = as_lines(dark_frames), as_lines(flat_frames)
    indices = (dark_index, flat_index)

    place = jnp.arange(DET, dtype=jnp.int32)
    first_low = jnp.where(upper, offset + 1, DET - offset)
    position = jnp.where(place >= first_low, place, place + DET).astype(jnp.float32)
    weight = jnp.clip((position - DET + 0.5 * spread) / spread, 0.0, 1.0)
    weight = jnp.where(upper, 1.0 - weight, weight)[None, :]
    scalars = jnp.stack([upper.astype(jnp.int32), first_low.astype(jnp.int32)])

    frequency = jnp.arange(DET + 1).astype(jnp.float32)
    stripe_line = ring_lines(impulse(stripe_gain, VIEWS))
    ramp_line = ring_lines(impulse(4.0 * frequency / STITCH * ramp_window, STITCH))
    stripe_high, stripe_low = bands(stripe_line, False)
    ramp_high, ramp_low = bands(ramp_line, True)

    groups = [list(range(half)), list(range(half, devices))]
    crossing = CROSS and DET // half >= 128
    sides = jnp.stack([upper.astype(jnp.int32), lax.axis_index("ang") % half])
    sides = sides if crossing else jnp.zeros_like(sides)

    def deliver(part, place):
        flip, turn = place // half, place % half
        if place == 0:
            return part
        pairs = [(src, (src // half ^ flip) * half + (src % half ^ turn)) for src in range(devices)]
        return lax.ppermute(part, "ang", pairs)

    sizes = CHUNKS if sum(CHUNKS) == rows else [rows]
    starts = [sum(sizes[:i]) for i in range(len(sizes))]
    fresh, crossed, parts = [], [], []
    for i, (start, size) in enumerate(zip(starts, sizes)):
        sent = prepare(scalars, indices, raw, dark, flat, weight, start, size, half)
        if i == 1:
            sent, stripe_high, stripe_low = lax.optimization_barrier((sent, stripe_high, stripe_low))
        columns = lax.all_to_all(sent, "ang", 0, 0, axis_index_groups=groups, tiled=True)
        if crossing and i >= 1:
            columns, crossed[i - 1][:HELD] = lax.optimization_barrier((columns, crossed[i - 1][:HELD]))
        fresh.append(destripe(sides, columns, stripe_high, stripe_low, devices, crossing))
        if crossing:
            crossed.append([deliver(part, half + place) for place, part in enumerate(fresh[i][half:])])
    for i, pieces in enumerate(fresh):
        if not crossing:
            parts.append([lax.all_to_all(pieces[0], "ang", 0, 0, tiled=True)])
            continue
        own = pieces[:half]
        if i + 1 < len(sizes) and KEPT > 0:
            own, crossed[i + 1][:KEPT] = lax.optimization_barrier((own, crossed[i + 1][:KEPT]))
        elif i + 1 < len(sizes):
            own, _ = lax.optimization_barrier((own, fresh[i + 1][0]))
        parts.append([deliver(part, place) for place, part in enumerate(own)] + crossed[i])
    done = []
    for pieces in parts[:-1]:
        done.append(ramp(sides, pieces, ramp_high, ramp_low))
    lines = ramp(sides, parts[-1], ramp_high, ramp_low, done, rows)
    views = VIEWS // devices
    filtered = lines.reshape(views, STITCH // 128, rows, 128).transpose(0, 2, 1, 3)
    return filtered.reshape(views, rows, STITCH)


def solution(mesh):
    in_specs = (
        P("ang", "slab", None),
        P(None, "slab", None),
        P(None, "slab", None),
        P("ang"),
        P("ang"),
        P(),
        P(),
        P(),
        P(),
    )
    out_specs = P("ang", "slab", None)
    return jax.shard_map(shards, mesh=mesh, in_specs=in_specs, out_specs=out_specs, check_vma=False)
```
